512 devices in a mesh: layer: 32 (over y, x, core), latent: 16 (over z).
Axes of the slice: x: 4, y: 4, z: 16, core: 2. Of those that a mesh axis runs over, the one named last changes fastest.
Arguments:
- layer_input: bfloat16 [32, 1024, 4096], P('layer', None, 'latent'), may hold values from -6 to 6
- enc_weight: bfloat16 [32, 4096, 2048], P('layer', None, 'latent'), may hold values from -0.09375 to 0.09375
- enc_bias: float32 [32, 2048], P('layer', 'latent'), may hold values from -3 to 3
- dec_weight: bfloat16 [32, 3, 2048, 4096], P('layer', None, None, 'latent'), may hold values from -0.25 to 0.25
- block_lists: int32 [32, 16, 8], P('layer'), may hold values from 0 to 15, as said below
- block_counts: int32 [32, 16], P('layer'), may hold values from 1 to 8, as said below
Outputs:
- rebuilt: bfloat16 [32, 1024, 4096], P('layer', None, 'latent')
The draws below stay inside these ranges and needn't reach their ends.
Inputs may be any that keep to these rules, and one draw needn't show every extreme that they name: `block_lists`: each list holds distinct block ids of one layer. `block_counts`: some entry equals 8 in every draw.
All inputs are finite; a program needn't handle non-finite values.
Results may differ from the reference program's by a relative error of at most 0.0055.
Values may be sent and summed in bfloat16 or wider, within the bound.
A program may use at most 128 MiB of HBM per device.

```python
import jax
import jax.numpy as jnp
from jax import lax

D = 4096
BLK = 128
TILE = 64
SPAN = 3
TOK = 1024
LAYERS = 32
BLOCKS = 16
LATR = 2048
KMAX = 8
TILES = 16


def draw_block_lists(key, part):
    keys = jax.random.split(key, LAYERS * TILES)
    orders = jax.vmap(lambda single: jax.random.permutation(single, BLOCKS))(keys)
    return orders[:, :KMAX].reshape(LAYERS, TILES, KMAX).astype(jnp.int32)


def draw_block_counts(key, part):
    counts = jax.random.randint(key, (LAYERS * TILES,), 1, KMAX + 1)
    where_full = jax.random.randint(jax.random.fold_in(key, 7), (), 0, LAYERS * TILES)
    counts = counts.at[where_full].set(KMAX)
    return counts.reshape(LAYERS, TILES).astype(jnp.int32)


def levels(key, shape, shards, smallest, high):
    level = 1.0
    for dim, blocks in shards:
        heights = jax.random.uniform(jax.random.fold_in(jax.random.fold_in(key, 6), dim), (blocks,), jnp.float32, smallest / len(shards), high / len(shards))
        level = level * jnp.repeat(jnp.exp(heights), shape[dim] // blocks).reshape((-1,) + (1,) * (len(shape) - 1 - dim))
    return level


def gaussian(stream_key, shape, scale, reach, pieces=(), dtype=jnp.bfloat16):
    array = scale * jax.random.normal(stream_key, shape, jnp.float32)
    if pieces:
        array = array * levels(stream_key, shape, pieces, -0.22, 0.18)
    return jnp.clip(array, -reach, reach).astype(dtype)


def setup_inputs(seed: int = 0) -> dict:
    seeds = jax.random.split(jax.random.key(seed), 7)
    return {
        "layer_input": gaussian(seeds[0], (LAYERS, TOK, D), 1.0, 6.0, ((0, 32), (2, 16))),
        "enc_weight": gaussian(seeds[1], (LAYERS, D, LATR), D ** -0.5, 0.09375, ((0, 32), (2, 16))),
        "enc_bias": gaussian(seeds[2], (LAYERS, LATR), 0.5, 3.0, ((0, 32), (1, 16)), jnp.float32),
        "dec_weight": gaussian(seeds[3], (LAYERS, SPAN, LATR, D), (LATR // 4) ** -0.5, 0.25, ((0, 32), (3, 16))),
        "block_lists": draw_block_lists(jax.random.fold_in(seeds[6], 71), 0),
        "block_counts": draw_block_counts(jax.random.fold_in(seeds[6], 71), 0),
    }


def reference(layer_input, enc_weight, enc_bias, dec_weight, block_lists, block_counts):
    slot_ids = jnp.arange(KMAX)
    block_ids = jnp.arange(BLOCKS)
    rebuilt = jnp.zeros((LAYERS, TOK, D), jnp.float32)
    for source in range(LAYERS):
        preact = jnp.dot(layer_input[source], enc_weight[source], preferred_element_type=jnp.float32) + enc_bias[source][None, :]
        matched = (block_lists[source][:, :, None] == block_ids[None, None, :]) & (slot_ids[None, :, None] < block_counts[source][:, None, None])
        live = jnp.any(matched, axis=1).astype(jnp.float32)
        row_mask = jnp.repeat(jnp.repeat(live, TILE, axis=0), BLK, axis=1)
        latent_act = (jnp.maximum(preact, 0.0) * row_mask).astype(jnp.bfloat16)
        for offset in range(SPAN):
            if source + offset < LAYERS:
                term = jnp.dot(latent_act, dec_weight[source, offset], preferred_element_type=jnp.float32)
                if offset > 0:
                    term = lax.optimization_barrier(term.astype(jnp.bfloat16)).astype(jnp.float32)
                rebuilt = rebuilt.at[source + offset].add(term)
    return rebuilt.astype(jnp.bfloat16)
```

```python
import jax
import jax.numpy as jnp
from jax import lax
from jax.experimental import pallas as pl
from jax.experimental.pallas import tpu as pltpu
from jax.sharding import PartitionSpec as P

MESH = pl.DeviceIdType.MESH
BF16, F32 = jnp.bfloat16, jnp.float32
PIECES = 4


def kernel(
    x_hbm, enc_hbm, bias_ref, dec_hbm, lists, counts, out_ref,
    xv, wbuf, wd, pd, rs_in, rs_out, act, cur, dense, own, late, arrived, slot_of,
    load_sem, w_send, w_recv, rs_send, rs_recv, ag_send, ag_recv, out_send, out_recv,
):
    n, depth, blk = wbuf.shape
    tiles, tile = n, own.shape[1]
    slots = lists.shape[1]
    per = slots // PIECES
    targets = wd.shape[0]
    layers = lax.axis_size("layer")
    me, layer = lax.axis_index("latent"), lax.axis_index("layer")
    half = n // 2

    def ring(k):
        return lax.rem(k + 2 * n, n)

    load_x = pltpu.make_async_copy(x_hbm, xv, load_sem.at[0])
    load_w = pltpu.make_async_copy(enc_hbm.at[pl.ds(depth * me, depth)], wbuf.at[me], load_sem.at[1])
    load_d = pltpu.make_async_copy(dec_hbm, wd, load_sem.at[2])
    load_x.start()
    load_w.start()
    load_d.start()

    barrier = pltpu.get_barrier_semaphore()

    @pl.loop(1, n)
    def _(d):
        pl.semaphore_signal(barrier, inc=1, device_id={"latent": ring(me + d)}, device_id_type=MESH)

    expected = n - 1
    for j in range(1, targets):
        for delta in (j, -j):
            there = (layer + delta >= 0) & (layer + delta < layers)

            @pl.when(there)
            def _():
                pl.semaphore_signal(barrier, inc=1, device_id={"layer": layer + delta}, device_id_type=MESH)

            expected = expected + there.astype(jnp.int32)
    pl.semaphore_wait(barrier, expected)

    def shift(i):
        far = half - (i + 1) // 2
        return jnp.where(lax.rem(i, 2) == 1, far, n - far)

    def w_copy(i):
        to = ring(me + shift(i))
        return pltpu.make_async_remote_copy(
            src_ref=enc_hbm.at[pl.ds(pl.multiple_of(depth * to, depth), depth)],
            dst_ref=wbuf.at[me],
            send_sem=w_send.at[i], recv_sem=w_recv.at[i],
            device_id={"latent": to}, device_id_type=MESH,
        )

    def w_arrival(i):
        source = ring(me - shift(i))
        return source, pltpu.make_async_remote_copy(
            src_ref=wbuf.at[source], dst_ref=wbuf.at[source],
            send_sem=w_send.at[i], recv_sem=w_recv.at[i],
            device_id={"latent": source}, device_id_type=MESH,
        )

    @pl.loop(0, n - 1)
    def _(i):
        w_copy(i).start()

    @pl.loop(0, tiles)
    def _(t):
        @pl.loop(0, n)
        def _(b):
            found = jnp.int32(-1)
            for s in range(slots):
                hit = (lists[t, s] == b) & (s < counts[0, t])
                found = jnp.where(hit, s, found)
            slot_of[t, b] = found

    load_x.wait()
    load_w.wait()
    rows = xv.shape[0]
    chunk = min(rows, 256)

    def encode(source, bias):
        @pl.loop(0, rows // chunk)
        def _(c):
            part = pl.ds(pl.multiple_of(chunk * c, chunk), chunk)
            value = jnp.dot(xv[part], wbuf[source], preferred_element_type=F32)
            pd[source, part] = value if bias is None else value + bias

    encode(me, bias_ref[...])

    @pl.loop(0, n - 1)
    def _(i):
        source, copy = w_arrival(i)
        copy.wait_recv()
        encode(source, None)

    def hops(piece, way):
        return half if (piece < PIECES // 2) == (way == 0) else half - 1

    def tile_rows(t):
        return pl.ds(pl.multiple_of(tile * t, tile), tile)

    def partial(t, s):
        return pd[lists[t, s], tile_rows(t)]

    def neighbour(way):
        return {"latent": ring(me + (1 if way == 0 else -1))}

    def rs_copy(step, piece, way):
        part = pl.ds(per * piece, per)
        return pltpu.make_async_remote_copy(
            src_ref=rs_out.at[way, step, part], dst_ref=rs_in.at[way, step, part],
            send_sem=rs_send.at[way, step, piece], recv_sem=rs_recv.at[way, step, piece],
            device_id=neighbour(way), device_id_type=MESH,
        )

    def rs_step(step, first, last):
        for piece in range(PIECES):
            for way in (0, 1):
                count = hops(piece, way)
                if last and count < half:
                    continue
                t = ring(me + count - step) if way == 0 else ring(me - count + step)
                if not first:
                    rs_copy(step - 1, piece, way).wait_recv()
                for s in range(per * piece, per * piece + per):
                    value = partial(t, s)
                    if not first:
                        value = value + rs_in[way, step - 1, s].astype(F32)
                    rs_out[way, step, s] = value.astype(BF16)
                rs_copy(step, piece, way).start()

    rs_step(0, True, False)

    @pl.loop(1, half - 1)
    def _(step):
        rs_step(step, False, False)

    rs_step(half - 1, False, True)

    def ag_copy(step, piece, way):
        part = pl.ds(per * piece, per)
        t = ring(me - step) if way == 0 else ring(me + step)
        return pltpu.make_async_remote_copy(
            src_ref=act.at[t, part], dst_ref=act.at[t, part],
            send_sem=ag_send.at[way, step, piece], recv_sem=ag_recv.at[way, step, piece],
            device_id=neighbour(way), device_id_type=MESH,
        )

    def ag_arrival(step, piece, way):
        part = pl.ds(per * piece, per)
        t = ring(me - 1 - step) if way == 0 else ring(me + 1 + step)
        return pltpu.make_async_remote_copy(
            src_ref=act.at[t, part], dst_ref=act.at[t, part],
            send_sem=ag_send.at[way, step, piece], recv_sem=ag_recv.at[way, step, piece],
            device_id=neighbour(way), device_id_type=MESH,
        )

    for piece in range(PIECES):
        for way in (0, 1):
            rs_copy(hops(piece, way) - 1, piece, way).wait_recv()
        for s in range(per * piece, per * piece + per):
            value = partial(me, s)
            for way in (0, 1):
                value = value + rs_in[way, hops(piece, way) - 1, s].astype(F32)
            value = jnp.where(s < counts[0, me], jnp.maximum(value, 0.0), 0.0)
            act[me, s] = value.astype(BF16)
        for way in (0, 1):
            ag_copy(0, piece, way).start()

    load_d.wait()

    def out_copy(j, t):
        return pltpu.make_async_remote_copy(
            src_ref=late.at[j - 1, t], dst_ref=arrived.at[j - 1, t],
            send_sem=out_send.at[j - 1, t], recv_sem=out_recv.at[j - 1, t],
            device_id={"layer": lax.rem(layer + j, layers)}, device_id_type=MESH,
        )

    def decode(group):
        for k, t in enumerate(group):
            cur[...] = act[t]
            for b in range(n):
                slot = slot_of[t, b]
                value = cur[jnp.maximum(slot, 0)]
                value = jnp.where(slot >= 0, value, jnp.zeros_like(value))
                dense[k * tile : (k + 1) * tile, b * blk : (b + 1) * blk] = value
        m = len(group) * tile
        for j in range(targets):
            value = jnp.dot(dense[:m], wd[j], preferred_element_type=F32)
            for k, t in enumerate(group):
                mine = value[k * tile : (k + 1) * tile]
                if j == 0:
                    own[t] = mine
                else:
                    late[j - 1, t] = mine.astype(BF16)
            if j > 0:
                @pl.when(layer + j < layers)
                def _():
                    for t in group:
                        out_copy(j, t).start()

    decode([me])

    def ag_step(step, last):
        for piece in range(PIECES):
            for way in (0, 1):
                ag_arrival(step, piece, way).wait_recv()
                if not last or hops(piece, way) == half:
                    ag_copy(step + 1, piece, way).start()
        decode([ring(me - 1 - step), ring(me + 1 + step)])

    @pl.loop(0, half - 2)
    def _(step):
        ag_step(step, False)

    ag_step(half - 2, True)
    for piece in range(PIECES):
        for way in (0, 1):
            if hops(piece, way) == half:
                ag_arrival(half - 1, piece, way).wait_recv()
    decode([ring(me + half)])

    for j in range(1, targets):
        @pl.when(layer < j)
        def _():
            arrived[j - 1] = jnp.zeros(arrived.shape[1:], BF16)

    @pl.loop(0, tiles)
    def _(i):
        t = ring(me + jnp.where(lax.rem(i, 2) == 1, (i + 1) // 2, n - i // 2))
        for j in range(1, targets):
            @pl.when(layer >= j)
            def _():
                out_copy(j, t).wait_recv()
        value = own[t]
        for j in range(1, targets):
            value = value + arrived[j - 1, t].astype(F32)
        out_ref[tile_rows(t)] = value.astype(BF16)

    @pl.loop(0, n - 1)
    def _(i):
        w_copy(i).wait_send()

    def drain(step, last):
        for piece in range(PIECES):
            for way in (0, 1):
                if not last or hops(piece, way) == half:
                    rs_copy(step, piece, way).wait_send()
                    ag_copy(step, piece, way).wait_send()

    @pl.loop(0, half - 1)
    def _(step):
        drain(step, False)

    drain(half - 1, True)

    @pl.loop(0, tiles)
    def _(t):
        for j in range(1, targets):
            @pl.when(layer + j < layers)
            def _():
                out_copy(j, t).wait_send()


def shards(layer_input, enc_weight, enc_bias, dec_weight, block_lists, block_counts):
    x, enc, dec = layer_input[0], enc_weight[0], dec_weight[0]
    tokens, depth = x.shape
    blk = enc.shape[1]
    targets, _, feats = dec.shape
    tiles, slots = block_lists.shape[1:]
    n = lax.axis_size("latent")
    tile, half = tokens // tiles, n // 2
    anywhere = pl.BlockSpec(memory_space=pl.ANY)
    vmem = pl.BlockSpec(memory_space=pltpu.VMEM)
    smem = pl.BlockSpec(memory_space=pltpu.SMEM)
    dma = pltpu.SemaphoreType.DMA
    out = pl.pallas_call(
        kernel,
        out_shape=jax.ShapeDtypeStruct((tokens, feats), BF16),
        in_specs=[anywhere, anywhere, vmem, anywhere, smem, smem],
        out_specs=vmem,
        scratch_shapes=[
            pltpu.VMEM((tokens, depth), BF16),
            pltpu.VMEM((n, depth, blk), BF16),
            pltpu.VMEM(dec.shape, BF16),
            pltpu.VMEM((n, tokens, blk), F32),
            pltpu.VMEM((2, half, slots, tile, blk), BF16),
            pltpu.VMEM((2, half, slots, tile, blk), BF16),
            pltpu.VMEM((tiles, slots, tile, blk), BF16),
            pltpu.VMEM((slots, tile, blk), BF16),
            pltpu.VMEM((2 * tile, n * blk), BF16),
            pltpu.VMEM((tiles, tile, feats), F32),
            pltpu.VMEM((targets - 1, tiles, tile, feats), BF16),
            pltpu.VMEM((targets - 1, tiles, tile, feats), BF16),
            pltpu.SMEM((tiles, n), jnp.int32),
            dma((3,)),
            dma((n - 1,)),
            dma((n - 1,)),
            dma((2, half, PIECES)),
            dma((2, half, PIECES)),
            dma((2, half, PIECES)),
            dma((2, half, PIECES)),
            dma((targets - 1, tiles)),
            dma((targets - 1, tiles)),
        ],
        compiler_params=pltpu.CompilerParams(
            collective_id=0, has_side_effects=True, vmem_limit_bytes=48 << 20
        ),
        cost_estimate=pl.CostEstimate(
            flops=2 * tokens * n * blk * (depth + targets * feats),
            bytes_accessed=2 * (x.size + 2 * enc.size + dec.size + tokens * feats),
            transcendentals=0,
        ),
        name="transcoder",
    )(x, enc, enc_bias, dec, block_lists[0], block_counts)
    return out[None]


def solution(mesh):
    placed = (
        P("layer", None, "latent"),
        P("layer", None, "latent"),
        P("layer", "latent"),
        P("layer", None, None, "latent"),
        P("layer", None, None),
        P("layer", None),
    )
    return jax.shard_map(
        shards, mesh=mesh, in_specs=placed, out_specs=P("layer", None, "latent"), check_vma=False
    )
```

```python
import jax
import jax.numpy as jnp
from jax import lax
from jax.experimental import pallas as pl
from jax.experimental.pallas import tpu as pltpu
from jax.sharding import PartitionSpec as P

MESH = pl.DeviceIdType.MESH
BF16, F32 = jnp.bfloat16, jnp.float32
PIECES = 4


def kernel(
    x_hbm, enc_hbm, bias_ref, dec_hbm, lists, counts, out_ref,
    xv, wbuf, wd, pd, rs_in, rs_out, act, cur, dense, own, late, arrived, slot_of,
    load_sem, w_send, w_recv, rs_send, rs_recv, ag_send, ag_recv, out_send, out_recv,
):
    n, depth, blk = wbuf.shape
    tiles, tile = n, own.shape[1]
    slots = lists.shape[0]
    per = slots // PIECES
    targets = wd.shape[0]
    layers = lax.axis_size("layer")
    me, layer = lax.axis_index("latent"), lax.axis_index("layer")
    half = n // 2

    def ring(k):
        return lax.rem(k + 2 * n, n)

    load_x = pltpu.make_async_copy(x_hbm, xv, load_sem.at[0])
    load_w = pltpu.make_async_copy(enc_hbm.at[pl.ds(depth * me, depth)], wbuf.at[me], load_sem.at[1])
    load_d = pltpu.make_async_copy(dec_hbm, wd, load_sem.at[2])
    load_x.start()
    load_w.start()
    load_d.start()

    barrier = pltpu.get_barrier_semaphore()

    @pl.loop(1, n)
    def _(d):
        pl.semaphore_signal(barrier, inc=1, device_id={"latent": ring(me + d)}, device_id_type=MESH)

    expected = n - 1
    for j in range(1, targets):
        for delta in (j, -j):
            there = (layer + delta >= 0) & (layer + delta < layers)

            @pl.when(there)
            def _():
                pl.semaphore_signal(barrier, inc=1, device_id={"layer": layer + delta}, device_id_type=MESH)

            expected = expected + there.astype(jnp.int32)
    pl.semaphore_wait(barrier, expected)

    def shift(i):
        far = half - (i + 1) // 2
        return jnp.where(lax.rem(i, 2) == 1, far, n - far)

    def w_copy(i):
        to = ring(me + shift(i))
        return pltpu.make_async_remote_copy(
            src_ref=enc_hbm.at[pl.ds(pl.multiple_of(depth * to, depth), depth)],
            dst_ref=wbuf.at[me],
            send_sem=w_send.at[i], recv_sem=w_recv.at[i],
            device_id={"latent": to}, device_id_type=MESH,
        )

    def w_arrival(i):
        source = ring(me - shift(i))
        return source, pltpu.make_async_remote_copy(
            src_ref=wbuf.at[source], dst_ref=wbuf.at[source],
            send_sem=w_send.at[i], recv_sem=w_recv.at[i],
            device_id={"latent": source}, device_id_type=MESH,
        )

    @pl.loop(0, n - 1)
    def _(i):
        w_copy(i).start()

    @pl.loop(0, tiles)
    def _(t):
        @pl.loop(0, n)
        def _(b):
            found = jnp.int32(-1)
            for s in range(slots):
                hit = (lists[s, t] == b) & (s < counts[0, t])
                found = jnp.where(hit, s, found)
            slot_of[t, b] = found

    load_x.wait()
    load_w.wait()
    rows = xv.shape[0]
    chunk = min(rows, 256)

    def encode(source, bias):
        @pl.loop(0, rows // chunk)
        def _(c):
            part = pl.ds(pl.multiple_of(chunk * c, chunk), chunk)
            value = jnp.dot(xv[part], wbuf[source], preferred_element_type=F32)
            pd[source, part] = value if bias is None else value + bias

    encode(me, bias_ref[...])

    @pl.loop(0, n - 1)
    def _(i):
        source, copy = w_arrival(i)
        copy.wait_recv()
        encode(source, None)

    def from_opposite(piece, way):
        return (piece < PIECES // 2) == (way == 0)

    def tile_rows(t):
        return pl.ds(pl.multiple_of(tile * t, tile), tile)

    def partial(t, s):
        return pd[lists[s, t], tile_rows(t)]

    def toward(way, count):
        return ring(me + count if way == 0 else me - count)

    def hop(source, target, sends, recvs, index, way, count):
        return pltpu.make_async_remote_copy(
            src_ref=source, dst_ref=target, send_sem=sends.at[index], recv_sem=recvs.at[index],
            device_id={"latent": toward(way, count)}, device_id_type=MESH,
        )

    def slots_of(piece):
        return range(per * piece, per * piece + per)

    def rs_copy(step, piece, way):
        part = pl.ds(per * piece, per)
        return hop(rs_out.at[way, step, part], rs_in.at[way, step, part], rs_send, rs_recv, (way, step, piece), way, 1)

    last = half - 1

    def rs_jump(piece, way):
        part = pl.ds(per * piece, per)
        return hop(rs_out.at[way, last, part], rs_in.at[way, last, part], rs_send, rs_recv, (way, last, piece), way, 2)

    for piece in range(PIECES):
        for way in (0, 1):
            if from_opposite(piece, way):
                for s in slots_of(piece):
                    rs_out[way, last, s] = partial(ring(me + half), s).astype(BF16)
                rs_jump(piece, way).start()

    def rs_step(step, before, joined):
        for piece in range(PIECES):
            for way in (0, 1):
                if before:
                    rs_copy(step - 1, piece, way).wait_recv()
                join = joined and from_opposite(piece, way)
                if join:
                    rs_jump(piece, way).wait_recv()
                for s in slots_of(piece):
                    value = partial(toward(way, last - step), s)
                    if before:
                        value = value + rs_in[way, step - 1, s].astype(F32)
                    if join:
                        value = value + rs_in[way, last, s].astype(F32)
                    rs_out[way, step, s] = value.astype(BF16)
                rs_copy(step, piece, way).start()

    rs_step(0, False, False)
    rs_step(1, True, True)

    @pl.loop(2, last)
    def _(step):
        rs_step(step, True, False)

    def act_copy(t, piece, index, way, count):
        here = act.at[t, pl.ds(per * piece, per)]
        return hop(here, here, ag_send, ag_recv, index, way, count)

    def ag_copy(step, piece, way):
        return act_copy(toward(1 - way, step), piece, (way, step, piece), way, 1)

    def ag_arrival(step, piece, way):
        return act_copy(toward(1 - way, step + 1), piece, (way, step, piece), way, 1)

    def ag_jump(piece, way):
        return act_copy(toward(1 - way, last - 1), piece, (way, last, piece), way, 2)

    def ag_jumped(piece, way):
        return act_copy(ring(me + half), piece, (way, last, piece), way, 2)

    for piece in range(PIECES):
        for way in (0, 1):
            rs_copy(last - 1, piece, way).wait_recv()
        for s in slots_of(piece):
            value = partial(me, s)
            for way in (0, 1):
                value = value + rs_in[way, last - 1, s].astype(F32)
            value = jnp.where(s < counts[0, me], jnp.maximum(value, 0.0), 0.0)
            act[me, s] = value.astype(BF16)
        for way in (0, 1):
            ag_copy(0, piece, way).start()

    load_d.wait()

    def out_copy(j, t):
        return pltpu.make_async_remote_copy(
            src_ref=late.at[j - 1, t], dst_ref=arrived.at[j - 1, t],
            send_sem=out_send.at[j - 1, t], recv_sem=out_recv.at[j - 1, t],
            device_id={"layer": lax.rem(layer + j, layers)}, device_id_type=MESH,
        )

    def decode(group):
        for k, t in enumerate(group):
            cur[...] = act[t]
            for b in range(n):
                slot = slot_of[t, b]
                value = cur[jnp.maximum(slot, 0)]
                value = jnp.where(slot >= 0, value, jnp.zeros_like(value))
                dense[k * tile : (k + 1) * tile, b * blk : (b + 1) * blk] = value
        m = len(group) * tile
        for j in range(targets):
            value = jnp.dot(dense[:m], wd[j], preferred_element_type=F32)
            for k, t in enumerate(group):
                mine = value[k * tile : (k + 1) * tile]
                if j == 0:
                    own[t] = mine
                else:
                    late[j - 1, t] = mine.astype(BF16)
            if j > 0:
                @pl.when(layer + j < layers)
                def _():
                    for t in group:
                        out_copy(j, t).start()

    decode([me])

    def ag_step(step, jump):
        for piece in range(PIECES):
            for way in (0, 1):
                ag_arrival(step, piece, way).wait_recv()
                ag_copy(step + 1, piece, way).start()
                if jump and from_opposite(piece, way):
                    ag_jump(piece, way).start()
        decode([toward(1, step + 1), toward(0, step + 1)])

    @pl.loop(0, last - 2)
    def _(step):
        ag_step(step, False)

    ag_step(last - 2, True)
    for piece in range(PIECES):
        for way in (0, 1):
            ag_arrival(last - 1, piece, way).wait_recv()
            if from_opposite(piece, way):
                ag_jumped(piece, way).wait_recv()
    decode([toward(1, last), toward(0, last), ring(me + half)])

    for j in range(1, targets):
        @pl.when(layer < j)
        def _():
            arrived[j - 1] = jnp.zeros(arrived.shape[1:], BF16)

    @pl.loop(0, tiles)
    def _(i):
        t = ring(me + jnp.where(lax.rem(i, 2) == 1, (i + 1) // 2, n - i // 2))
        for j in range(1, targets):
            @pl.when(layer >= j)
            def _():
                out_copy(j, t).wait_recv()
        value = own[t]
        for j in range(1, targets):
            value = value + arrived[j - 1, t].astype(F32)
        out_ref[tile_rows(t)] = value.astype(BF16)

    @pl.loop(0, n - 1)
    def _(i):
        w_copy(i).wait_send()

    @pl.loop(0, last)
    def _(step):
        for piece in range(PIECES):
            for way in (0, 1):
                rs_copy(step, piece, way).wait_send()
                ag_copy(step, piece, way).wait_send()

    for piece in range(PIECES):
        for way in (0, 1):
            if from_opposite(piece, way):
                rs_jump(piece, way).wait_send()
                ag_jump(piece, way).wait_send()

    @pl.loop(0, tiles)
    def _(t):
        for j in range(1, targets):
            @pl.when(layer + j < layers)
            def _():
                out_copy(j, t).wait_send()


def shards(layer_input, enc_weight, enc_bias, dec_weight, block_lists, block_counts):
    x, enc, dec = layer_input[0], enc_weight[0], dec_weight[0]
    tokens, depth = x.shape
    blk = enc.shape[1]
    targets, _, feats = dec.shape
    tiles, slots = block_lists.shape[1:]
    n = lax.axis_size("latent")
    tile, half = tokens // tiles, n // 2
    hbm = pl.BlockSpec(memory_space=pltpu.HBM)
    vmem = pl.BlockSpec(memory_space=pltpu.VMEM)
    smem = pl.BlockSpec(memory_space=pltpu.SMEM)
    dma = pltpu.SemaphoreType.DMA
    out = pl.pallas_call(
        kernel,
        out_shape=jax.ShapeDtypeStruct((tokens, feats), BF16),
        in_specs=[hbm, hbm, vmem, hbm, smem, smem],
        out_specs=vmem,
        scratch_shapes=[
            pltpu.VMEM((tokens, depth), BF16),
            pltpu.VMEM((n, depth, blk), BF16),
            pltpu.VMEM(dec.shape, BF16),
            pltpu.VMEM((n, tokens, blk), F32),
            pltpu.VMEM((2, half, slots, tile, blk), BF16),
            pltpu.VMEM((2, half, slots, tile, blk), BF16),
            pltpu.VMEM((tiles, slots, tile, blk), BF16),
            pltpu.VMEM((slots, tile, blk), BF16),
            pltpu.VMEM((3 * tile, n * blk), BF16),
            pltpu.VMEM((tiles, tile, feats), F32),
            pltpu.VMEM((targets - 1, tiles, tile, feats), BF16),
            pltpu.VMEM((targets - 1, tiles, tile, feats), BF16),
            pltpu.SMEM((tiles, n), jnp.int32),
            dma((3,)),
            dma((n - 1,)),
            dma((n - 1,)),
            dma((2, half, PIECES)),
            dma((2, half, PIECES)),
            dma((2, half, PIECES)),
            dma((2, half, PIECES)),
            dma((targets - 1, tiles)),
            dma((targets - 1, tiles)),
        ],
        compiler_params=pltpu.CompilerParams(
            collective_id=0, has_side_effects=True, vmem_limit_bytes=67000000
        ),
        cost_estimate=pl.CostEstimate(
            flops=2 * tokens * n * blk * (depth + targets * feats),
            bytes_accessed=2 * (x.size + 2 * enc.size + dec.size + tokens * feats),
            transcendentals=0,
        ),
        name="transcoder",
    )(x, enc, enc_bias, dec, block_lists[0].T, block_counts)
    return out[None]


def solution(mesh):
    placed = (
        P("layer", None, "latent"),
        P("layer", None, "latent"),
        P("layer", "latent"),
        P("layer", None, None, "latent"),
        P("layer", None, None),
        P("layer", None),
    )
    return jax.shard_map(
        shards, mesh=mesh, in_specs=placed, out_specs=P("layer", None, "latent"), check_vma=False
    )
```

```python
import jax
import jax.numpy as jnp
from jax import lax
from jax.experimental import pallas as pl
from jax.experimental.pallas import tpu as pltpu
from jax.sharding import PartitionSpec as P

MESH = pl.DeviceIdType.MESH
BF16, F32 = jnp.bfloat16, jnp.float32
PIECES = 4


def kernel(
    x_hbm, enc_hbm, bias_ref, dec_hbm, lists, counts, own_out, arrived,
    xv, wbuf, wd, pd, rs_in, rs_out, act, cur, dense, own, late, slot_of,
    load_sem, w_send, w_recv, rs_send, rs_recv, ag_send, ag_recv, out_send, out_recv, own_sem,
):
    n, depth, blk = wbuf.shape
    tiles, tile = n, own.shape[1]
    slots = lists.shape[0]
    per = slots // PIECES
    targets = wd.shape[0]
    layers = lax.axis_size("layer")
    me, layer = lax.axis_index("latent"), lax.axis_index("layer")
    half = n // 2

    def ring(k):
        return lax.rem(k + 2 * n, n)

    load_x = pltpu.make_async_copy(x_hbm, xv, load_sem.at[0])
    load_w = pltpu.make_async_copy(enc_hbm.at[pl.ds(depth * me, depth)], wbuf.at[me], load_sem.at[1])
    load_d = pltpu.make_async_copy(dec_hbm, wd, load_sem.at[2])
    load_x.start()
    load_w.start()
    load_d.start()

    barrier = pltpu.get_barrier_semaphore()

    @pl.loop(1, n)
    def _(d):
        pl.semaphore_signal(barrier, inc=1, device_id={"latent": ring(me + d)}, device_id_type=MESH)

    expected = n - 1
    for j in range(1, targets):
        for delta in (j, -j):
            there = (layer + delta >= 0) & (layer + delta < layers)

            @pl.when(there)
            def _():
                pl.semaphore_signal(barrier, inc=1, device_id={"layer": layer + delta}, device_id_type=MESH)

            expected = expected + there.astype(jnp.int32)
    pl.semaphore_wait(barrier, expected)

    def shift(i):
        far = half - (i + 1) // 2
        return jnp.where(lax.rem(i, 2) == 1, far, n - far)

    def w_copy(i):
        to = ring(me + shift(i))
        return pltpu.make_async_remote_copy(
            src_ref=enc_hbm.at[pl.ds(pl.multiple_of(depth * to, depth), depth)],
            dst_ref=wbuf.at[me],
            send_sem=w_send.at[i], recv_sem=w_recv.at[i],
            device_id={"latent": to}, device_id_type=MESH,
        )

    def w_arrival(i):
        source = ring(me - shift(i))
        return source, pltpu.make_async_remote_copy(
            src_ref=wbuf.at[source], dst_ref=wbuf.at[source],
            send_sem=w_send.at[i], recv_sem=w_recv.at[i],
            device_id={"latent": source}, device_id_type=MESH,
        )

    @pl.loop(0, n - 1)
    def _(i):
        w_copy(i).start()

    @pl.loop(0, tiles)
    def _(t):
        @pl.loop(0, n)
        def _(b):
            found = jnp.int32(-1)
            for s in range(slots):
                hit = (lists[s, t] == b) & (s < counts[0, t])
                found = jnp.where(hit, s, found)
            slot_of[t, b] = found

    load_x.wait()
    load_w.wait()
    rows = xv.shape[0]
    chunk = min(rows, 256)

    def encode(source, bias):
        @pl.loop(0, rows // chunk)
        def _(c):
            part = pl.ds(pl.multiple_of(chunk * c, chunk), chunk)
            value = jnp.dot(xv[part], wbuf[source], preferred_element_type=F32)
            pd[source, part] = value if bias is None else value + bias

    encode(me, bias_ref[...])

    @pl.loop(0, n - 1)
    def _(i):
        source, copy = w_arrival(i)
        copy.wait_recv()
        encode(source, None)

    def from_opposite(piece, way):
        return (piece < PIECES // 2) == (way == 0)

    def tile_rows(t):
        return pl.ds(pl.multiple_of(tile * t, tile), tile)

    def partial(t, s):
        return pd[lists[s, t], tile_rows(t)]

    def toward(way, count):
        return ring(me + count if way == 0 else me - count)

    def hop(source, target, sends, recvs, index, way, count):
        return pltpu.make_async_remote_copy(
            src_ref=source, dst_ref=target, send_sem=sends.at[index], recv_sem=recvs.at[index],
            device_id={"latent": toward(way, count)}, device_id_type=MESH,
        )

    def slots_of(piece):
        return range(per * piece, per * piece + per)

    def rs_copy(step, piece, way):
        part = pl.ds(per * piece, per)
        return hop(rs_out.at[way, step, part], rs_in.at[way, step, part], rs_send, rs_recv, (way, step, piece), way, 1)

    last = half - 1

    def rs_jump(piece, way):
        part = pl.ds(per * piece, per)
        return hop(rs_out.at[way, last, part], rs_in.at[way, last, part], rs_send, rs_recv, (way, last, piece), way, 2)

    for piece in range(PIECES):
        for way in (0, 1):
            if from_opposite(piece, way):
                for s in slots_of(piece):
                    rs_out[way, last, s] = partial(ring(me + half), s).astype(BF16)
                rs_jump(piece, way).start()

    def rs_step(step, before, joined):
        for piece in range(PIECES):
            for way in (0, 1):
                if before:
                    rs_copy(step - 1, piece, way).wait_recv()
                join = joined and from_opposite(piece, way)
                if join:
                    rs_jump(piece, way).wait_recv()
                for s in slots_of(piece):
                    value = partial(toward(way, last - step), s)
                    if before:
                        value = value + rs_in[way, step - 1, s].astype(F32)
                    if join:
                        value = value + rs_in[way, last, s].astype(F32)
                    rs_out[way, step, s] = value.astype(BF16)
                rs_copy(step, piece, way).start()

    rs_step(0, False, False)
    rs_step(1, True, True)

    @pl.loop(2, last)
    def _(step):
        rs_step(step, True, False)

    def act_copy(t, piece, index, way, count):
        here = act.at[t, pl.ds(per * piece, per)]
        return hop(here, here, ag_send, ag_recv, index, way, count)

    def ag_copy(step, piece, way):
        return act_copy(toward(1 - way, step), piece, (way, step, piece), way, 1)

    def ag_arrival(step, piece, way):
        return act_copy(toward(1 - way, step + 1), piece, (way, step, piece), way, 1)

    def ag_jump(piece, way):
        return act_copy(toward(1 - way, last - 1), piece, (way, last, piece), way, 2)

    def ag_jumped(piece, way):
        return act_copy(ring(me + half), piece, (way, last, piece), way, 2)

    for piece in range(PIECES):
        for way in (0, 1):
            rs_copy(last - 1, piece, way).wait_recv()
        for s in slots_of(piece):
            value = partial(me, s)
            for way in (0, 1):
                value = value + rs_in[way, last - 1, s].astype(F32)
            value = jnp.where(s < counts[0, me], jnp.maximum(value, 0.0), 0.0)
            act[me, s] = value.astype(BF16)
        for way in (0, 1):
            ag_copy(0, piece, way).start()

    load_d.wait()

    def out_copy(j, t):
        return pltpu.make_async_remote_copy(
            src_ref=late.at[j - 1, t], dst_ref=arrived.at[j - 1, t],
            send_sem=out_send.at[j - 1, t], recv_sem=out_recv.at[j - 1, t],
            device_id={"layer": lax.rem(layer + j, layers)}, device_id_type=MESH,
        )

    def own_copy(t):
        return pltpu.make_async_copy(own.at[t], own_out.at[t], own_sem.at[t])

    def decode(group):
        for k, t in enumerate(group):
            cur[...] = act[t]

            @pl.loop(0, n, unroll=2)
            def _(b):
                slot = slot_of[t, b]
                value = cur[jnp.maximum(slot, 0)]
                value = jnp.where(slot >= 0, value, jnp.zeros_like(value))
                dense[k * tile : (k + 1) * tile, pl.ds(pl.multiple_of(b * blk, blk), blk)] = value

        def term(j):
            return jnp.dot(dense[...], wd[j], preferred_element_type=F32)

        @pl.loop(1, targets)
        def _(j):
            value = term(j)
            for k, t in enumerate(group):
                late[j - 1, t] = value[k * tile : (k + 1) * tile].astype(BF16)

            @pl.when(layer + j < layers)
            def _():
                for t in group:
                    out_copy(j, t).start()

        value = term(0)
        for k, t in enumerate(group):
            own[t] = value[k * tile : (k + 1) * tile]
            own_copy(t).start()

    @pl.loop(0, half)
    def _(step):
        for piece in range(PIECES):
            for way in (0, 1):
                @pl.when(step < last)
                def _():
                    ag_arrival(step, piece, way).wait_recv()

                @pl.when(step < last - 1)
                def _():
                    ag_copy(step + 1, piece, way).start()

                if from_opposite(piece, way):
                    @pl.when(step == last - 2)
                    def _():
                        ag_jump(piece, way).start()

                    @pl.when(step == last)
                    def _():
                        ag_jumped(piece, way).wait_recv()

        decode([toward(1, step + 1), toward(0, lax.rem(step + 1, half))])

    @pl.loop(0, tiles)
    def _(t):
        own_copy(t).wait()
        for j in range(1, targets):
            @pl.when(layer >= j)
            def _():
                out_copy(j, t).wait_recv()

    @pl.loop(0, n - 1)
    def _(i):
        w_copy(i).wait_send()

    @pl.loop(0, last)
    def _(step):
        for piece in range(PIECES):
            for way in (0, 1):
                rs_copy(step, piece, way).wait_send()
                ag_copy(step, piece, way).wait_send()

    for piece in range(PIECES):
        for way in (0, 1):
            if from_opposite(piece, way):
                rs_jump(piece, way).wait_send()
                ag_jump(piece, way).wait_send()

    @pl.loop(0, tiles)
    def _(t):
        for j in range(1, targets):
            @pl.when(layer + j < layers)
            def _():
                out_copy(j, t).wait_send()


def shards(layer_input, enc_weight, enc_bias, dec_weight, block_lists, block_counts):
    x, enc, dec = layer_input[0], enc_weight[0], dec_weight[0]
    tokens, depth = x.shape
    blk = enc.shape[1]
    targets, _, feats = dec.shape
    tiles, slots = block_lists.shape[1:]
    n = lax.axis_size("latent")
    tile, half = tokens // tiles, n // 2
    hbm = pl.BlockSpec(memory_space=pltpu.HBM)
    vmem = pl.BlockSpec(memory_space=pltpu.VMEM)
    smem = pl.BlockSpec(memory_space=pltpu.SMEM)
    dma = pltpu.SemaphoreType.DMA
    own, arrived = pl.pallas_call(
        kernel,
        out_shape=[
            jax.ShapeDtypeStruct((tiles, tile, feats), F32),
            jax.ShapeDtypeStruct((targets - 1, tiles, tile, feats), BF16),
        ],
        in_specs=[hbm, hbm, vmem, hbm, smem, smem],
        out_specs=[hbm, hbm],
        scratch_shapes=[
            pltpu.VMEM((tokens, depth), BF16),
            pltpu.VMEM((n, depth, blk), BF16),
            pltpu.VMEM(dec.shape, BF16),
            pltpu.VMEM((n, tokens, blk), F32),
            pltpu.VMEM((2, half, slots, tile, blk), BF16),
            pltpu.VMEM((2, half, slots, tile, blk), BF16),
            pltpu.VMEM((tiles, slots, tile, blk), BF16),
            pltpu.VMEM((slots, tile, blk), BF16),
            pltpu.VMEM((2 * tile, n * blk), BF16),
            pltpu.VMEM((tiles, tile, feats), F32),
            pltpu.VMEM((targets - 1, tiles, tile, feats), BF16),
            pltpu.SMEM((tiles, n), jnp.int32),
            dma((3,)),
            dma((n - 1,)),
            dma((n - 1,)),
            dma((2, half, PIECES)),
            dma((2, half, PIECES)),
            dma((2, half, PIECES)),
            dma((2, half, PIECES)),
            dma((targets - 1, tiles)),
            dma((targets - 1, tiles)),
            dma((tiles,)),
        ],
        compiler_params=pltpu.CompilerParams(
            collective_id=0, has_side_effects=True, vmem_limit_bytes=40 << 20
        ),
        cost_estimate=pl.CostEstimate(
            flops=2 * tokens * n * blk * (depth + targets * feats),
            bytes_accessed=2 * (x.size + 2 * enc.size + dec.size + tokens * feats),
            transcendentals=0,
        ),
        name="transcoder",
    )(*(pltpu.with_memory_space_constraint(a, pltpu.HBM) for a in (x, enc, enc_bias, dec, block_lists[0].T, block_counts)))
    layer = lax.axis_index("layer")
    rebuilt = own
    for j in range(1, targets):
        term = arrived[j - 1].astype(F32)
        rebuilt = rebuilt + jnp.where(layer >= j, term, 0.0)
    return rebuilt.astype(BF16).reshape(1, tokens, feats)


def solution(mesh):
    placed = (
        P("layer", None, "latent"),
        P("layer", None, "latent"),
        P("layer", "latent"),
        P("layer", None, None, "latent"),
        P("layer", None, None),
        P("layer", None),
    )
    return jax.shard_map(
        shards, mesh=mesh, in_specs=placed, out_specs=P("layer", None, "latent"), check_vma=False
    )
```

```python
import jax
import jax.numpy as jnp
from jax import lax
from jax.experimental import pallas as pl
from jax.experimental.pallas import tpu as pltpu
from jax.sharding import PartitionSpec as P

MESH = pl.DeviceIdType.MESH
BF16, F32 = jnp.bfloat16, jnp.float32
PIECES = 4


def kernel(
    x_hbm, enc_hbm, bias_ref, dec_hbm, lists, counts, own_out, arrived,
    xv, wbuf, wd, pd, rs_in, rs_out, act, cur, dense, own, late, slot_of,
    load_sem, w_send, w_recv, rs_send, rs_recv, ag_send, ag_recv, out_send, out_recv, own_sem,
):
    n, depth, blk = wbuf.shape
    tiles, tile = n, own.shape[1]
    slots = lists.shape[0]
    per = slots // PIECES
    targets = wd.shape[0]
    layers = lax.axis_size("layer")
    me, layer = lax.axis_index("latent"), lax.axis_index("layer")
    half = n // 2

    def ring(k):
        k = jnp.where(k >= n, k - n, k)
        return jnp.where(k < 0, k + n, k)

    load_x = pltpu.make_async_copy(x_hbm, xv, load_sem.at[0])
    load_w = pltpu.make_async_copy(enc_hbm.at[pl.ds(depth * me, depth)], wbuf.at[me], load_sem.at[1])
    load_d = pltpu.make_async_copy(dec_hbm, wd, load_sem.at[2])
    load_x.start()
    load_w.start()
    load_d.start()

    barrier = pltpu.get_barrier_semaphore()

    @pl.loop(1, n)
    def _(d):
        pl.semaphore_signal(barrier, inc=1, device_id={"latent": ring(me + d)}, device_id_type=MESH)

    expected = n - 1
    for j in range(1, targets):
        for delta in (j, -j):
            there = (layer + delta >= 0) & (layer + delta < layers)

            @pl.when(there)
            def _():
                pl.semaphore_signal(barrier, inc=1, device_id={"layer": layer + delta}, device_id_type=MESH)

            expected = expected + there.astype(jnp.int32)
    pl.semaphore_wait(barrier, expected)

    def shift(i):
        far = half - (i + 1) // 2
        return jnp.where(lax.rem(i, 2) == 1, far, n - far)

    def w_copy(i):
        to = ring(me + shift(i))
        return pltpu.make_async_remote_copy(
            src_ref=enc_hbm.at[pl.ds(pl.multiple_of(depth * to, depth), depth)],
            dst_ref=wbuf.at[me],
            send_sem=w_send.at[i], recv_sem=w_recv.at[i],
            device_id={"latent": to}, device_id_type=MESH,
        )

    def w_arrival(i):
        source = ring(me - shift(i))
        return source, pltpu.make_async_remote_copy(
            src_ref=wbuf.at[source], dst_ref=wbuf.at[source],
            send_sem=w_send.at[i], recv_sem=w_recv.at[i],
            device_id={"latent": source}, device_id_type=MESH,
        )

    @pl.loop(0, n - 1)
    def _(i):
        w_copy(i).start()

    @pl.loop(0, tiles)
    def _(t):
        @pl.loop(0, n)
        def _(b):
            found = jnp.int32(-1)
            for s in range(slots):
                hit = (lists[s, t] == b) & (s < counts[0, t])
                found = jnp.where(hit, s, found)
            slot_of[t, b] = found

    load_x.wait()
    load_w.wait()
    rows = xv.shape[0]
    chunk = min(rows, 256)

    def encode(source, bias):
        @pl.loop(0, rows // chunk)
        def _(c):
            part = pl.ds(pl.multiple_of(chunk * c, chunk), chunk)
            value = jnp.dot(xv[part], wbuf[source], preferred_element_type=F32)
            pd[source, part] = value if bias is None else value + bias

    encode(me, bias_ref[...])

    @pl.loop(0, n - 1)
    def _(i):
        source, copy = w_arrival(i)
        copy.wait_recv()
        encode(source, None)

    def from_opposite(piece, way):
        return (piece < PIECES // 2) == (way == 0)

    def tile_rows(t):
        return pl.ds(pl.multiple_of(tile * t, tile), tile)

    def partial(t, s):
        return pd[lists[s, t], tile_rows(t)]

    def toward(way, count):
        return ring(me + count if way == 0 else me - count)

    beside = [[toward(way, count) for count in (1, 2)] for way in (0, 1)]

    def hop(source, target, sends, recvs, index, way, count):
        return pltpu.make_async_remote_copy(
            src_ref=source, dst_ref=target, send_sem=sends.at[index], recv_sem=recvs.at[index],
            device_id={"latent": beside[way][count - 1]}, device_id_type=MESH,
        )

    def slots_of(piece):
        return range(per * piece, per * piece + per)

    def rs_copy(step, piece, way):
        part = pl.ds(per * piece, per)
        return hop(rs_out.at[way, step, part], rs_in.at[way, step, part], rs_send, rs_recv, (way, step, piece), way, 1)

    last = half - 1

    def rs_jump(piece, way):
        part = pl.ds(per * piece, per)
        return hop(rs_out.at[way, last, part], rs_in.at[way, last, part], rs_send, rs_recv, (way, last, piece), way, 2)

    for piece in range(PIECES):
        for way in (0, 1):
            if from_opposite(piece, way):
                for s in slots_of(piece):
                    rs_out[way, last, s] = partial(ring(me + half), s).astype(BF16)
                rs_jump(piece, way).start()

    def rs_step(step, before, joined):
        for piece in range(PIECES):
            for way in (0, 1):
                if before:
                    rs_copy(step - 1, piece, way).wait_recv()
                join = joined and from_opposite(piece, way)
                if join:
                    rs_jump(piece, way).wait_recv()
                for s in slots_of(piece):
                    value = partial(toward(way, last - step), s)
                    if before:
                        value = value + rs_in[way, step - 1, s].astype(F32)
                    if join:
                        value = value + rs_in[way, last, s].astype(F32)
                    rs_out[way, step, s] = value.astype(BF16)
                rs_copy(step, piece, way).start()

    rs_step(0, False, False)
    rs_step(1, True, True)

    @pl.loop(2, last)
    def _(step):
        rs_step(step, True, False)

    def act_copy(t, piece, index, way, count):
        here = act.at[t, pl.ds(per * piece, per)]
        return hop(here, here, ag_send, ag_recv, index, way, count)

    def ag_copy(step, piece, way):
        return act_copy(toward(1 - way, step), piece, (way, step, piece), way, 1)

    def ag_arrival(step, piece, way):
        return act_copy(toward(1 - way, step + 1), piece, (way, step, piece), way, 1)

    def ag_jump(piece, way):
        return act_copy(toward(1 - way, last - 1), piece, (way, last, piece), way, 2)

    def ag_jumped(piece, way):
        return act_copy(ring(me + half), piece, (way, last, piece), way, 2)

    for piece in range(PIECES):
        for way in (0, 1):
            rs_copy(last - 1, piece, way).wait_recv()
        for s in slots_of(piece):
            value = partial(me, s)
            for way in (0, 1):
                value = value + rs_in[way, last - 1, s].astype(F32)
            value = jnp.where(s < counts[0, me], jnp.maximum(value, 0.0), 0.0)
            act[me, s] = value.astype(BF16)
        for way in (0, 1):
            ag_copy(0, piece, way).start()

    load_d.wait()

    def out_copy(j, t):
        return pltpu.make_async_remote_copy(
            src_ref=late.at[j - 1, t], dst_ref=arrived.at[j - 1, t],
            send_sem=out_send.at[j - 1, t], recv_sem=out_recv.at[j - 1, t],
            device_id={"layer": jnp.where(layer + j >= layers, layer + j - layers, layer + j)}, device_id_type=MESH,
        )

    def own_copy(t):
        return pltpu.make_async_copy(own.at[t], own_out.at[t], own_sem.at[t])

    def decode(group):
        for k, t in enumerate(group):
            cur[...] = act[t]

            @pl.loop(0, n, unroll=2)
            def _(b):
                slot = slot_of[t, b]
                value = cur[jnp.maximum(slot, 0)]
                value = jnp.where(slot >= 0, value, jnp.zeros_like(value))
                dense[k * tile : (k + 1) * tile, pl.ds(pl.multiple_of(b * blk, blk), blk)] = value

        def term(j):
            return jnp.dot(dense[...], wd[j], preferred_element_type=F32)

        @pl.loop(1, targets)
        def _(j):
            value = term(j)
            for k, t in enumerate(group):
                late[j - 1, t] = value[k * tile : (k + 1) * tile].astype(BF16)

            @pl.when(layer + j < layers)
            def _():
                for t in group:
                    out_copy(j, t).start()

        value = term(0)
        for k, t in enumerate(group):
            own[t] = value[k * tile : (k + 1) * tile]
            own_copy(t).start()

    @pl.loop(0, half)
    def _(step):
        for piece in range(PIECES):
            for way in (0, 1):
                @pl.when(step < last)
                def _():
                    ag_arrival(step, piece, way).wait_recv()

                @pl.when(step < last - 1)
                def _():
                    ag_copy(step + 1, piece, way).start()

                if from_opposite(piece, way):
                    @pl.when(step == last - 2)
                    def _():
                        ag_jump(piece, way).start()

                    @pl.when(step == last)
                    def _():
                        ag_jumped(piece, way).wait_recv()

        decode([toward(1, step + 1), toward(0, jnp.where(step == last, 0, step + 1))])

    @pl.loop(0, tiles)
    def _(t):
        own_copy(t).wait()
        for j in range(1, targets):
            @pl.when(layer >= j)
            def _():
                out_copy(j, t).wait_recv()

    @pl.loop(0, n - 1)
    def _(i):
        w_copy(i).wait_send()

    @pl.loop(0, last)
    def _(step):
        for piece in range(PIECES):
            for way in (0, 1):
                rs_copy(step, piece, way).wait_send()
                ag_copy(step, piece, way).wait_send()

    for piece in range(PIECES):
        for way in (0, 1):
            if from_opposite(piece, way):
                rs_jump(piece, way).wait_send()
                ag_jump(piece, way).wait_send()

    @pl.loop(0, tiles)
    def _(t):
        for j in range(1, targets):
            @pl.when(layer + j < layers)
            def _():
                out_copy(j, t).wait_send()


def shards(layer_input, enc_weight, enc_bias, dec_weight, block_lists, block_counts):
    x, enc, dec = layer_input[0], enc_weight[0], dec_weight[0]
    tokens, depth = x.shape
    blk = enc.shape[1]
    targets, _, feats = dec.shape
    tiles, slots = block_lists.shape[1:]
    n = lax.axis_size("latent")
    tile, half = tokens // tiles, n // 2
    hbm = pl.BlockSpec(memory_space=pltpu.HBM)
    vmem = pl.BlockSpec(memory_space=pltpu.VMEM)
    smem = pl.BlockSpec(memory_space=pltpu.SMEM)
    dma = pltpu.SemaphoreType.DMA
    own, arrived = pl.pallas_call(
        kernel,
        out_shape=[
            jax.ShapeDtypeStruct((tiles, tile, feats), F32),
            jax.ShapeDtypeStruct((targets - 1, tiles, tile, feats), BF16),
        ],
        in_specs=[hbm, hbm, vmem, hbm, smem, smem],
        out_specs=[hbm, hbm],
        scratch_shapes=[
            pltpu.VMEM((tokens, depth), BF16),
            pltpu.VMEM((n, depth, blk), BF16),
            pltpu.VMEM(dec.shape, BF16),
            pltpu.VMEM((n, tokens, blk), F32),
            pltpu.VMEM((2, half, slots, tile, blk), BF16),
            pltpu.VMEM((2, half, slots, tile, blk), BF16),
            pltpu.VMEM((tiles, slots, tile, blk), BF16),
            pltpu.VMEM((slots, tile, blk), BF16),
            pltpu.VMEM((2 * tile, n * blk), BF16),
            pltpu.VMEM((tiles, tile, feats), F32),
            pltpu.VMEM((targets - 1, tiles, tile, feats), BF16),
            pltpu.SMEM((tiles, n), jnp.int32),
            dma((3,)),
            dma((n - 1,)),
            dma((n - 1,)),
            dma((2, half, PIECES)),
            dma((2, half, PIECES)),
            dma((2, half, PIECES)),
            dma((2, half, PIECES)),
            dma((targets - 1, tiles)),
            dma((targets - 1, tiles)),
            dma((tiles,)),
        ],
        compiler_params=pltpu.CompilerParams(
            collective_id=0, has_side_effects=True, vmem_limit_bytes=40 << 20
        ),
        cost_estimate=pl.CostEstimate(
            flops=2 * tokens * n * blk * (depth + targets * feats),
            bytes_accessed=2 * (x.size + 2 * enc.size + dec.size + tokens * feats),
            transcendentals=0,
        ),
        name="transcoder",
    )(*(pltpu.with_memory_space_constraint(a, pltpu.HBM) for a in (x, enc, enc_bias, dec, block_lists[0].T, block_counts)))
    layer = lax.axis_index("layer")
    rebuilt = own
    for j in range(1, targets):
        term = arrived[j - 1].astype(F32)
        rebuilt = rebuilt + jnp.where(layer >= j, term, 0.0)
    return rebuilt.astype(BF16).reshape(1, tokens, feats)


def solution(mesh):
    placed = (
        P("layer", None, "latent"),
        P("layer", None, "latent"),
        P("layer", "latent"),
        P("layer", None, None, "latent"),
        P("layer", None, None),
        P("layer", None),
    )
    return jax.shard_map(
        shards, mesh=mesh, in_specs=placed, out_specs=P("layer", None, "latent"), check_vma=False
    )
```
